32 devices in a mesh: src: 8 (over y, x, core), tgt: 4 (over z).
Axes of the slice: x: 2, y: 2, z: 4, core: 2. Of those that a mesh axis runs over, the one named last changes fastest.
Arguments:
- src_coords: float32 [3, 49152], P(None, 'src'), may hold values from 0 to 1, as said below
- tgt_coords: float32 [3, 24576], P(None, 'tgt'), may hold values from 0 to 1
- src_scaling: float32 [32, 49152], P('tgt', 'src'), may hold values from 0.25 to 4
- src_mass: float32 [32, 49152], P('tgt', 'src'), may hold values from 0.25 to 4
- tgt_mass: float32 [32, 24576], P(None, 'tgt'), may hold values from 0.25 to 4
Outputs:
- new_src_scaling: float32 [32, 49152], P('tgt', 'src')
- tgt_scaling: float32 [32, 24576], P('src', 'tgt')
The draws below stay inside these ranges and needn't reach their ends.
Inputs may be any that keep to these rules, and one draw needn't show every extreme that they name: `src_coords`: source points lie in the unit cube.
All inputs are finite; a program needn't handle non-finite values.
Results may differ from the reference program's by a relative error of at most 0.00036.
Values may be sent and summed in bfloat16 or wider, within the bound.
No kernel may reach another device: no remote copies, remote signals or barrier semaphores. Data moves between devices by JAX's collectives and lax.ppermute only.
A program may use at most 64 MiB of HBM per device.

```python
import math
import jax
import jax.numpy as jnp
from jax import lax

WEIGHTS = 32
NS = 49152
NT = 24576


def draw_src_coords(key, part):
    base = jax.random.uniform(key, (3, NS), jnp.float32)
    first = 0.6 * base[0:1]
    return jnp.concatenate([first, base[1:]], axis=0)


def steps_of(stream_key, dims, shards, least, high):
    factor_of, own = 1.0, jax.random.fold_in(stream_key, 6)
    for axis_at, shards_of in shards:
        draws = jnp.exp(jax.random.uniform(jax.random.fold_in(own, axis_at), (shards_of,), jnp.float32, least / len(shards), high / len(shards)))
        factor_of = factor_of * jnp.repeat(draws, dims[axis_at] // shards_of).reshape([-1 if axis == axis_at else 1 for axis in range(len(dims))])
    return factor_of


def setup_inputs(seed: int = 0) -> dict:
    keys = jax.random.split(jax.random.key(seed), 6)
    src_coords = draw_src_coords(jax.random.fold_in(keys[5], 71), 0)
    tgt_coords = jnp.clip(1.0 * jax.random.uniform(keys[1], (3, NT), jnp.float32) ** steps_of(keys[1], (3, NT), ((1, 4),), -0.2, 0.2), 0.0, 1.0)
    src_scaling = jnp.clip(jnp.exp(math.log(4.0) - 2.7725887 * jax.random.uniform(keys[2], (WEIGHTS, NS), jnp.float32) ** steps_of(keys[2], (WEIGHTS, NS), ((0, 4), (1, 8)), -0.2, 0.2)), 0.25, 4.0)
    src_mass = jnp.clip(jnp.exp(math.log(4.0) - 2.7725887 * jax.random.uniform(keys[3], (WEIGHTS, NS), jnp.float32) ** steps_of(keys[3], (WEIGHTS, NS), ((0, 4), (1, 8)), -0.2, 0.2)), 0.25, 4.0)
    tgt_mass = jnp.clip(jnp.exp(math.log(4.0) - 2.7725887 * jax.random.uniform(keys[4], (WEIGHTS, NT), jnp.float32) ** steps_of(keys[4], (WEIGHTS, NT), ((1, 4),), -0.2, 0.2)), 0.25, 4.0)
    return {"src_coords": src_coords, "tgt_coords": tgt_coords, "src_scaling": src_scaling, "src_mass": src_mass, "tgt_mass": tgt_mass}


def kernel_block(xb, yt):
    dist = (xb[0][:, None] - yt[0][None, :]) ** 2
    dist = dist + (xb[1][:, None] - yt[1][None, :]) ** 2
    dist = dist + (xb[2][:, None] - yt[2][None, :]) ** 2
    return (180.0 * jnp.exp(-100.0 * dist)).astype(jnp.bfloat16)


def reference(src_coords, tgt_coords, src_scaling, src_mass, tgt_mass):
    block = 512
    count = NS // block
    xs_blocks = src_coords.reshape(3, count, block).transpose(1, 0, 2)
    src_low = src_scaling.astype(jnp.bfloat16)
    u_blocks = src_low.reshape(WEIGHTS, count, block).transpose(1, 0, 2)

    def col_step(carry, items):
        xb, ub = items
        kern = kernel_block(xb, tgt_coords)
        return carry + jnp.dot(ub, kern, preferred_element_type=jnp.float32), None

    col_sums, _ = lax.scan(col_step, jnp.zeros((WEIGHTS, NT), jnp.float32), (xs_blocks, u_blocks))
    tgt_scaling = tgt_mass / (col_sums / NS)
    tgt_low = tgt_scaling.astype(jnp.bfloat16)

    def row_step(xb):
        kern = kernel_block(xb, tgt_coords)
        return jnp.dot(tgt_low, kern.T, preferred_element_type=jnp.float32)

    rows = lax.map(row_step, xs_blocks)
    row_sums = rows.transpose(1, 0, 2).reshape(WEIGHTS, NS)
    new_src_scaling = src_mass / (row_sums / NT)
    return new_src_scaling, tgt_scaling
```

```python
import functools
import math

import jax
import jax.numpy as jnp
from jax import lax
from jax.experimental import pallas as pl
from jax.experimental.pallas import tpu as pltpu
from jax.sharding import PartitionSpec as P

LOG2E = 1.4426950408889634
FEATURES = 32


def pieces(value):
    out = []
    for _ in range(3):
        part = lax.reduce_precision(value, 8, 7)
        out.append(part)
        value = value - part
    return out


def features(coords, is_src):
    rate = 100.0 * LOG2E
    shifted = coords - 0.5
    norm = -rate * jnp.sum(shifted * shifted, axis=0)
    scaled = shifted
    if is_src:
        norm = norm + math.log2(180.0)
        scaled = (2.0 * rate) * shifted
    hi, mid, lo = pieces(scaled)
    one = jnp.ones_like(norm)
    own = pieces(norm)
    if is_src:
        rows = [hi, hi, mid, hi, lo, mid]
        ends = own + [one] * 3
    else:
        rows = [hi, mid, hi, lo, hi, mid]
        ends = [one] * 3 + own
    full = jnp.concatenate(rows + [jnp.stack(ends)], axis=0)
    pad = FEATURES - full.shape[0]
    return jnp.pad(full, ((0, pad), (0, 0))).astype(jnp.bfloat16)


def tile_of(size, most):
    tile = min(size, most)
    while size % tile:
        tile -= 128
    return tile


def sum_kernel(tk, tn, left_ref, right_ref, scale_ref, out_ref):
    weights = scale_ref.shape[0]
    ks = left_ref.shape[0] // tk
    ns = right_ref.shape[1] // tn

    @pl.loop(0, ns)
    def _(n):
        cols = pl.ds(pl.multiple_of(n * tn, tn), tn)
        right = right_ref[:, cols]

        def body(k, acc):
            rows = pl.ds(pl.multiple_of(k * tk, tk), tk)
            power = jnp.dot(left_ref[rows, :], right, preferred_element_type=jnp.float32)
            kern = jnp.exp2(power).astype(jnp.bfloat16)
            return acc + jnp.dot(scale_ref[:, rows], kern, preferred_element_type=jnp.float32)

        zero = jnp.zeros((weights, tn), jnp.float32)
        out_ref[:, cols] = lax.fori_loop(0, ks, body, zero)


def weighted_sums(left, right, scale):
    points, terms = left.shape[0], right.shape[1]
    weights = scale.shape[0]
    tk, tn = tile_of(points, 1024), tile_of(terms, 2048)
    whole = pl.BlockSpec(memory_space=pltpu.VMEM)
    return pl.pallas_call(
        functools.partial(sum_kernel, tk, tn),
        out_shape=jax.ShapeDtypeStruct((weights, terms), jnp.float32),
        in_specs=[whole] * 3,
        out_specs=whole,
        compiler_params=pltpu.CompilerParams(vmem_limit_bytes=48 * 1024 * 1024),
        cost_estimate=pl.CostEstimate(
            flops=2 * (weights + FEATURES) * points * terms,
            transcendentals=points * terms,
            bytes_accessed=4 * weights * (points + terms),
        ),
    )(left, right, scale)


def swap(x, axis, mask):
    size = lax.axis_size(axis)
    return lax.ppermute(x, axis, [(i, i ^ mask) for i in range(size)])


def gather_rows(x, axis):
    size, me = lax.axis_size(axis), lax.axis_index(axis)
    out = jnp.zeros((size,) + x.shape, x.dtype)
    out = lax.dynamic_update_index_in_dim(out, x, me, 0)
    for step in range(1, size):
        got = lax.ppermute(x, axis, [(i, (i + step) % size) for i in range(size)])
        out = lax.dynamic_update_index_in_dim(out, got, (me + size - step) % size, 0)
    return out.reshape((size * x.shape[0],) + x.shape[1:])


def scatter_sum(x, axis):
    size, me = lax.axis_size(axis), lax.axis_index(axis)
    x = x.reshape((size, x.shape[0] // size) + x.shape[1:])
    bit = 0
    while (1 << bit) < size:
        x = x.reshape((x.shape[0] // 2, 2) + x.shape[1:])
        mine = (me >> bit) & 1
        keep = lax.dynamic_index_in_dim(x, mine, 1, False)
        send = lax.dynamic_index_in_dim(x, 1 - mine, 1, False)
        x = keep + swap(send, axis, 1 << bit)
        bit += 1
    return x[0]


def on_device(src_coords, tgt_coords, src_scaling, src_mass, tgt_mass):
    src_pts = src_coords.shape[1]
    tgt_pts = tgt_coords.shape[1]
    weights = tgt_mass.shape[0]
    total_src = src_pts * lax.axis_size("src")
    total_tgt = tgt_pts * lax.axis_size("tgt")
    share = weights // lax.axis_size("src")

    src_low = gather_rows(src_scaling.astype(jnp.bfloat16), "tgt")
    src_feat = features(src_coords, True)
    tgt_feat = features(tgt_coords, False)

    col_terms = weighted_sums(src_feat.T, tgt_feat, src_low)
    col_part = scatter_sum(col_terms, "src")
    mass = lax.dynamic_slice_in_dim(tgt_mass, lax.axis_index("src") * share, share, 0)
    tgt_scaling = mass / (col_part / total_src)
    tgt_low = gather_rows(tgt_scaling.astype(jnp.bfloat16), "src")

    row_terms = weighted_sums(tgt_feat.T, src_feat, tgt_low)
    row_part = scatter_sum(row_terms, "tgt")
    new_src_scaling = src_mass / (row_part / total_tgt)
    return (new_src_scaling, tgt_scaling)


def solution(mesh):
    placed = (P(None, "src"), P(None, "tgt"), P("tgt", "src"), P("tgt", "src"), P(None, "tgt"))
    return jax.shard_map(
        on_device,
        mesh=mesh,
        in_specs=placed,
        out_specs=(P("tgt", "src"), P("src", "tgt")),
        check_vma=False,
    )
```

```python
import functools
import math

import jax
import jax.numpy as jnp
from jax import lax
from jax.experimental import pallas as pl
from jax.experimental.pallas import tpu as pltpu
from jax.sharding import PartitionSpec as P


LOG2E = 1.4426950408889634
FEATURES = 32


def pieces(value):
    out = []
    for _ in range(3):
        part = lax.reduce_precision(value, 8, 7)
        out.append(part)
        value = value - part
    return out


def features(coords, is_src):
    rate = 100.0 * LOG2E
    shifted = coords - 0.5
    norm = -rate * jnp.sum(shifted * shifted, axis=0)
    scaled = shifted
    if is_src:
        norm = norm + math.log2(180.0)
        scaled = (2.0 * rate) * shifted
    hi, mid, lo = pieces(scaled)
    one = jnp.ones_like(norm)
    own = pieces(norm)
    if is_src:
        rows = [hi, hi, mid, hi, lo, mid]
        ends = own + [one] * 3
    else:
        rows = [hi, mid, hi, lo, hi, mid]
        ends = [one] * 3 + own
    full = jnp.concatenate(rows + [jnp.stack(ends)], axis=0)
    pad = FEATURES - full.shape[0]
    return jnp.pad(full, ((0, pad), (0, 0))).astype(jnp.bfloat16)


def tile_of(size, most):
    tile = min(size, most)
    while size % tile:
        tile -= 128
    return tile


def sum_kernel(tk, tn, first, left_ref, right_ref, scale_ref, *refs):
    parts, out_ref = refs[:-1], refs[-1]
    weights = scale_ref.shape[0]
    held = sum(part.shape[0] for part in parts)
    ks = (left_ref.shape[0] - held) // tk
    ns = out_ref.shape[1] // tn

    @pl.loop(0, ns)
    def _(n):
        here = pl.multiple_of(n * tn, tn)
        cols = pl.ds(pl.multiple_of(first + here, 128), tn)
        right = right_ref[:, cols]

        def body(k, acc):
            rows = pl.ds(pl.multiple_of(held + k * tk, 128), tk)
            power = jnp.dot(left_ref[rows, :], right, preferred_element_type=jnp.float32)
            kern = jnp.exp2(power).astype(jnp.bfloat16)
            return acc + jnp.dot(scale_ref[:, rows], kern, preferred_element_type=jnp.float32)

        total = jnp.zeros((weights, tn), jnp.float32)
        at = 0
        for part in parts:
            rows = slice(at, at + part.shape[0])
            total = total + jnp.dot(scale_ref[:, rows], part[:, cols], preferred_element_type=jnp.float32)
            at = rows.stop
        out_ref[:, pl.ds(here, tn)] = lax.fori_loop(0, ks, body, total)


WHOLE = pl.BlockSpec(memory_space=pltpu.VMEM)
KERNEL_BYTES = 8 * 1024 * 1024


def weighted_sums(left, right, scale, first, terms, parts=()):
    points = left.shape[0]
    fresh = points - sum(part.shape[0] for part in parts)
    weights = scale.shape[0]
    tk, tn = tile_of(fresh, 1024), tile_of(terms, 2048)
    return pl.pallas_call(
        functools.partial(sum_kernel, tk, tn, first),
        out_shape=jax.ShapeDtypeStruct((weights, terms), jnp.float32),
        in_specs=[WHOLE] * (3 + len(parts)),
        out_specs=WHOLE,
        compiler_params=pltpu.CompilerParams(vmem_limit_bytes=KERNEL_BYTES),
        cost_estimate=pl.CostEstimate(
            flops=16 * (weights * points + FEATURES * fresh) * terms,
            transcendentals=fresh * terms,
            bytes_accessed=4 * weights * (points + terms),
        ),
    )(left, right, scale, *parts)


def power_kernel(tn, first, left_ref, right_ref, out_ref):
    left = left_ref[pl.ds(first, out_ref.shape[0]), :]

    @pl.loop(0, out_ref.shape[1] // tn)
    def _(n):
        cols = pl.ds(pl.multiple_of(n * tn, tn), tn)
        power = jnp.dot(left, right_ref[:, cols], preferred_element_type=jnp.float32)
        out_ref[:, cols] = jnp.exp2(power).astype(jnp.bfloat16)


def kernel_rows(left, right, first, rows):
    terms = right.shape[1]
    return pl.pallas_call(
        functools.partial(power_kernel, tile_of(terms, 3072), first),
        out_shape=jax.ShapeDtypeStruct((rows, terms), jnp.bfloat16),
        in_specs=[WHOLE] * 2,
        out_specs=WHOLE,
        compiler_params=pltpu.CompilerParams(vmem_limit_bytes=KERNEL_BYTES),
        cost_estimate=pl.CostEstimate(
            flops=16 * FEATURES * rows * terms,
            transcendentals=rows * terms,
            bytes_accessed=2 * rows * terms,
        ),
    )(left, right)


def swap(x, axis, mask):
    size = lax.axis_size(axis)
    return lax.ppermute(x, axis, [(i, i ^ mask) for i in range(size)])


def gather_xor(x, axis):
    size = lax.axis_size(axis)
    return jnp.concatenate([x] + [swap(x, axis, step) for step in range(1, size)], axis=0)


def gather_double(x, axis, upper, lower):
    x = x[None]
    for bit in range(len(upper)):
        got = swap(x, axis, 1 << bit)
        both = jnp.zeros((2,) + x.shape, x.dtype)
        both = lax.dynamic_update_index_in_dim(both, x, upper[bit], 0)
        both = lax.dynamic_update_index_in_dim(both, got, lower[bit], 0)
        x = both.reshape((2 * x.shape[0],) + x.shape[1:])
    return x


def scatter_halve(x, axis, size, mine, other):
    x = x.reshape((size, x.shape[0] // size) + x.shape[1:])
    for bit in range(len(mine)):
        x = x.reshape((x.shape[0] // 2, 2) + x.shape[1:])
        keep = lax.dynamic_index_in_dim(x, mine[bit], 1, False)
        send = lax.dynamic_index_in_dim(x, other[bit], 1, False)
        got = swap(send, axis, 1 << bit)
        x = keep + got
    return x[0]


def scatter_direct(x, axis, blocks):
    size = len(blocks)
    x = x.reshape((size, x.shape[0] // size) + x.shape[1:])
    out = lax.dynamic_index_in_dim(x, blocks[0], 0, False)
    for step in range(1, size):
        got = swap(lax.dynamic_index_in_dim(x, blocks[step], 0, False), axis, step)
        out = out + got
    return out


def stack_kernel(in_ref, out_ref, wide_ref):
    blocks, rows = in_ref.shape[0], in_ref.shape[1]
    for q in range(blocks):
        wide_ref[q * rows:(q + 1) * rows, :] = in_ref[q].astype(jnp.float32)
    out_ref[...] = wide_ref[...].astype(out_ref.dtype)


def stack_rows(x):
    rows, points = x.shape[0] * x.shape[1], x.shape[2]
    return pl.pallas_call(
        stack_kernel,
        out_shape=jax.ShapeDtypeStruct((rows, points), x.dtype),
        in_specs=[WHOLE],
        out_specs=WHOLE,
        scratch_shapes=[pltpu.VMEM((rows, points), jnp.float32)],
        compiler_params=pltpu.CompilerParams(vmem_limit_bytes=KERNEL_BYTES),
    )(x)


def cuts(size):
    unit = size // 4
    if size % 4 or unit % 128:
        return [(0, size)]
    return [(0, 2 * unit), (2 * unit, unit), (3 * unit, unit)]


def held_rows(points):
    rows = points // 8
    return [(q * rows, rows) for q in range(4)] if rows % 128 == 0 else []


def on_device(src_coords, tgt_coords, src_scaling, src_mass, tgt_mass):
    src_pts = src_coords.shape[1]
    tgt_pts = tgt_coords.shape[1]
    weights = tgt_mass.shape[0]
    src_size, tgt_size = lax.axis_size("src"), lax.axis_size("tgt")
    total_src, total_tgt = src_pts * src_size, tgt_pts * tgt_size
    share = weights // src_size

    me, at = lax.axis_index("src"), lax.axis_index("tgt")
    bits = range((src_size - 1).bit_length())
    turned = me ^ (at * (src_size // tgt_size))
    places = [
        [(turned >> bit) & 1 for bit in bits],
        [1 - ((turned >> bit) & 1) for bit in bits],
        [(me >> bit) & 1 for bit in bits],
        [1 - ((me >> bit) & 1) for bit in bits],
        [at ^ step for step in range(tgt_size)],
        [me * share],
    ]
    places = jax.tree.map(lambda place: place.astype(jnp.uint32), places)

    src_low = gather_xor(src_scaling.astype(jnp.bfloat16), "tgt")
    src_feat = features(src_coords, True)
    tgt_feat = features(tgt_coords, False)
    places, src_low, src_rows, tgt_rows = lax.optimization_barrier(
        (places, src_low, src_feat.T, tgt_feat.T)
    )
    mine, other, upper, lower, blocks, row = places

    col_terms = weighted_sums(src_rows, tgt_feat, src_low, 0, tgt_pts)
    col_part = scatter_halve(col_terms, "src", src_size, mine, other)
    mass = lax.dynamic_slice_in_dim(tgt_mass, row[0], share, 0)
    tgt_scaling = mass / (col_part / total_src)
    tgt_low = stack_rows(gather_double(tgt_scaling.astype(jnp.bfloat16), "src", upper, lower))

    parts = []
    for first, count in held_rows(tgt_pts):
        parts.append(kernel_rows(tgt_rows, src_feat, first, count))
    new = []
    for first, count in cuts(src_pts):
        row_terms = weighted_sums(tgt_rows, src_feat, tgt_low, first, count, parts)
        row_part = scatter_direct(row_terms, "tgt", blocks)
        new.append(src_mass[:, first:first + count] / (row_part / total_tgt))
    return (jnp.concatenate(new, axis=1), tgt_scaling)


def solution(mesh):
    placed = (P(None, "src"), P(None, "tgt"), P("tgt", "src"), P("tgt", "src"), P(None, "tgt"))

    return jax.shard_map(
        on_device,
        mesh=mesh,
        in_specs=placed,
        out_specs=(P("tgt", "src"), P("src", "tgt")),
        check_vma=False,
    )
```
